256 devices in a mesh: grid: 16 (over y, x), band: 8 (over z), pole: 2 (over core).
Axes of the slice: x: 4, y: 4, z: 8, core: 2. Of those that a mesh axis runs over, the one named last changes fastest.
Arguments:
- solution: bfloat16 [2, 512, 64, 16, 256], P('pole', 'band', 'grid'), may hold values from -6 to 6
- proj_vals: bfloat16 [256, 128, 2048], P('grid'), may hold values from -0.125 to 0.125
- slot_offset: int32 [256], P('grid'), may hold values from 0 to 14336
- slot_block: int32 [16, 16], replicated, may hold values from 0 to 127, as said below
- proj_coef: float32 [128, 128], P('grid'), may hold values from -0.015625 to 0.015625
- pole_weight: float32 [2], P('pole'), may hold values from 0.25 to 1
- proj_atom: int32 [128, 128], P('grid'), may hold values from -1 to 55, as said below
Outputs:
- forces: float32 [3, 896], P(None, 'grid')
The draws below stay inside these ranges and needn't reach their ends.
Inputs may be any that keep to these rules, and one draw needn't show every extreme that they name: `slot_block`: the blocks of one brick's row differ; at most 2 of them belong to one owner (block // 8); in every draw one owner gets exactly 2 blocks from every brick. `proj_atom`: each block of owner o holds 18 projectors of each of 7 of o's atoms, each of o's atoms in exactly one block, and -1 in its other positions.
All inputs are finite; a program needn't handle non-finite values.
Results may differ from the reference program's by a relative error of at most 0.013.
Values may be sent and summed in bfloat16 or wider, within the bound.
No kernel may reach another device: no remote copies, remote signals or barrier semaphores. Data moves between devices by JAX's collectives and lax.ppermute only.
A program may use at most 128 MiB of HBM per device.

```python
import jax
import jax.numpy as jnp
from jax import lax

PLX = 4
NY = 16
NZ = 256
PROJ = 128
PROJ_ATOM = 18
ATOM_BLK = 7
WIN = 2048
SLOTS = 16
BLK_OWN = 8
BRICKS = 16
CAP = 2
NX = 64
POLES = 2
COLS_T = 512
NBLK = 128
ATOM_OWN = 56
ATOMS = 896
BRICK_SLOTS = 256


def draw_slot_block(key, part):
    key_owner, key_score, key_shift, key_order = jax.random.split(jax.random.fold_in(key, 11), 4)
    full_owner = jax.random.randint(key_owner, (), 0, BRICKS)
    seat_ids = jnp.arange(BRICKS * CAP, dtype=jnp.int32)
    seat_owner = seat_ids // CAP
    noise_draw = jax.random.randint(key_score, (BRICKS, BRICKS * CAP), 0, 2 ** 20)
    scores = noise_draw * (BRICKS * CAP) + seat_ids[None, :] + jnp.where(seat_owner == full_owner, 2 ** 28, 0)[None, :]
    _, chosen = lax.top_k(scores, SLOTS)
    owners = chosen // CAP
    seat_rank = chosen % CAP
    shifts = jax.random.randint(key_shift, (BRICKS, BRICKS), 0, BLK_OWN)
    local_block = (seat_rank + jnp.take_along_axis(shifts, owners, axis=1)) % BLK_OWN
    blocks = owners * BLK_OWN + local_block
    order_draw = jax.random.randint(key_order, (BRICKS, SLOTS), 0, 2 ** 20) * SLOTS + jnp.arange(SLOTS, dtype=jnp.int32)[None, :]
    shuffle = jnp.argsort(order_draw, axis=1)
    return jnp.take_along_axis(blocks, shuffle, axis=1).astype(jnp.int32)


def draw_proj_atom(key, part):
    key_atoms, key_places = jax.random.split(jax.random.fold_in(key, 23), 2)
    atom_draw = jax.random.randint(key_atoms, (BRICKS, ATOM_OWN), 0, 2 ** 20) * ATOM_OWN + jnp.arange(ATOM_OWN, dtype=jnp.int32)[None, :]
    shuffle = jnp.argsort(atom_draw, axis=1).astype(jnp.int32)
    blocks = jnp.arange(NBLK, dtype=jnp.int32)
    owners = blocks // BLK_OWN
    local_block = blocks % BLK_OWN
    places = jnp.arange(PROJ, dtype=jnp.int32)
    atom_slot = local_block[:, None] * ATOM_BLK + jnp.minimum(places // PROJ_ATOM, ATOM_BLK - 1)[None, :]
    atoms = shuffle[owners[:, None], atom_slot]
    values = jnp.where(places[None, :] < ATOM_BLK * PROJ_ATOM, atoms, -1)
    place_draw = jax.random.randint(key_places, (NBLK, PROJ), 0, 2 ** 20) * PROJ + places[None, :]
    order = jnp.argsort(place_draw, axis=1)
    return jnp.take_along_axis(values, order, axis=1).astype(jnp.int32)


def plant(result, stream_key, smallest, top_value):
    shape = result.shape
    spot = [jax.random.randint(jax.random.fold_in(stream_key, axis), (), 0, shape[axis]) for axis in range(len(shape))]
    result = result.at[tuple(spot)].set(smallest)
    longest = shape.index(max(shape))
    spot[longest] = (spot[longest] + 1) % shape[longest]
    return result.at[tuple(spot)].set(top_value)


def levels(key, shape, cuts, smallest, high):
    loudness = 1.0
    for dim, shards_of in cuts:
        heights = jax.random.uniform(jax.random.fold_in(jax.random.fold_in(key, 6), dim), (shards_of,), jnp.float32, smallest / len(cuts), high / len(cuts))
        loudness = loudness * jnp.repeat(jnp.exp(heights), shape[dim] // shards_of).reshape((-1,) + (1,) * (len(shape) - 1 - dim))
    return loudness


def centred(rng, extent, scale, limit, pieces=(), held_as=jnp.bfloat16):
    entries = scale * jax.random.normal(rng, extent, jnp.float32)
    if pieces:
        entries = entries * levels(rng, extent, pieces, -0.22, 0.18)
    return jnp.clip(entries, -limit, limit).astype(held_as)


def setup_inputs(seed: int = 0) -> dict:
    streams_of = jax.random.split(jax.random.key(seed), 8)
    solution = centred(streams_of[0], (POLES, COLS_T, NX, NY, NZ), 1.0, 6.0, ((0, 2), (1, 8), (2, 16)))
    proj_vals = centred(streams_of[1], (BRICK_SLOTS, PROJ, WIN), WIN ** -0.5, 0.125, ((0, 16),))
    slot_offset = plant(jax.random.randint(streams_of[2], (BRICK_SLOTS,), 0, PLX * NY * NZ - WIN + 1), jax.random.fold_in(streams_of[2], 1), 0, PLX * NY * NZ - WIN).astype(jnp.int32)
    slot_block = draw_slot_block(jax.random.fold_in(streams_of[7], 71), 0)
    proj_coef = centred(streams_of[4], (NBLK, PROJ), 0.003, 0.015625, ((0, 16),), jnp.float32)
    pole_weight = jnp.clip(0.25 + 0.75 * jax.random.uniform(streams_of[5], (POLES,), jnp.float32) ** levels(streams_of[5], (POLES,), ((0, 2),), -0.2, 0.2), 0.25, 1.0)
    proj_atom = draw_proj_atom(jax.random.fold_in(streams_of[7], 71), 0)
    return dict(solution=solution, proj_vals=proj_vals, slot_offset=slot_offset, slot_block=slot_block, proj_coef=proj_coef, pole_weight=pole_weight, proj_atom=proj_atom)


def derivative(upper, lower):
    return ((upper.astype(jnp.float32) - lower.astype(jnp.float32)) * 0.5).astype(jnp.bfloat16)


def build_fields(extended):
    middle = extended[:, :, 1:-1]
    grad_x = derivative(extended[:, :, 2:], extended[:, :, :-2])
    grad_y = derivative(jnp.roll(middle, -1, axis=3), jnp.roll(middle, 1, axis=3))
    grad_z = derivative(jnp.roll(middle, -1, axis=4), jnp.roll(middle, 1, axis=4))
    stacked = jnp.stack([middle, grad_x, grad_y, grad_z], axis=0)
    return stacked.reshape(4 * middle.shape[0] * middle.shape[1], -1)


def reference(solution, proj_vals, slot_offset, slot_block, proj_coef, pole_weight, proj_atom):
    height = 4 * POLES * COLS_T

    def brick_step(running, brick_index):
        plane_start = (brick_index * PLX).astype(jnp.int32)
        middle = lax.dynamic_slice_in_dim(solution, plane_start, PLX, 2)
        previous = lax.dynamic_slice_in_dim(solution, ((plane_start - 1 + NX) % NX).astype(jnp.int32), 1, 2)
        following = lax.dynamic_slice_in_dim(solution, ((plane_start + PLX) % NX).astype(jnp.int32), 1, 2)
        fields = build_fields(jnp.concatenate([previous, middle, following], axis=2))
        slot_start = (brick_index * SLOTS).astype(jnp.int32)
        projector = lax.dynamic_slice_in_dim(proj_vals, slot_start, SLOTS, 0)
        offsets = lax.dynamic_slice_in_dim(slot_offset, slot_start, SLOTS, 0)
        block_ids = lax.dynamic_index_in_dim(slot_block, brick_index, 0, keepdims=False)

        def slot_step(inner, triple):
            block_vals, offset, block_id = triple
            window = lax.dynamic_slice_in_dim(fields, offset.astype(jnp.int32), WIN, 1)
            partial_value = lax.dot_general(window, block_vals, (((1,), (1,)), ((), ())), preferred_element_type=jnp.float32).astype(jnp.bfloat16)
            partial_value = lax.optimization_barrier(partial_value).astype(jnp.float32)
            return inner.at[block_id].add(partial_value), None

        running, _ = lax.scan(slot_step, running, (projector, offsets, block_ids))
        return running, None

    start_coef = jnp.zeros((NBLK, height, PROJ), jnp.float32)
    coefficients, _ = lax.scan(brick_step, start_coef, jnp.arange(BRICKS, dtype=jnp.int32))
    shaped = coefficients.reshape(NBLK, 4, POLES, COLS_T, PROJ)
    weighted = jnp.einsum("bpci,bxpci,p->xbi", shaped[:, 0], shaped[:, 1:], pole_weight.astype(jnp.float32))
    force_terms = -2.0 * weighted * proj_coef[None]
    onehot = (proj_atom.reshape(BRICKS, BLK_OWN, PROJ)[:, :, :, None] == jnp.arange(ATOM_OWN, dtype=jnp.int32)).astype(jnp.float32)
    forces = jnp.einsum("xobi,obia->xoa", force_terms.reshape(3, BRICKS, BLK_OWN, PROJ), onehot)
    return forces.reshape(3, ATOMS)
```

```python
import jax
import jax.numpy as jnp
from jax import lax
from jax.experimental import pallas as pl
from jax.experimental.pallas import tpu as pltpu
from jax.sharding import PartitionSpec as P

ATOM_OWN = 56
LANES = 128
BF = jnp.bfloat16
F32 = jnp.float32


def shifted(p_ref, shift, chunks):
    lane = lax.broadcasted_iota(jnp.int32, (p_ref.shape[1], LANES), 1)
    low = lane < shift
    rolled = [
        pltpu.roll(p_ref[0, :, j * LANES : (j + 1) * LANES], shift, 1) for j in range(chunks)
    ]
    zero = jnp.zeros_like(rolled[0])
    pieces = [jnp.where(low, zero, rolled[0])]
    for j in range(1, chunks):
        pieces.append(jnp.where(low, rolled[j - 1], rolled[j]))
    pieces.append(jnp.where(low, rolled[-1], zero))
    return jnp.concatenate(pieces, axis=1)


def window_of(field_ref, first, chunks):
    last = field_ref.shape[0] - 1
    parts = [field_ref[first + j] for j in range(chunks)]
    parts.append(field_ref[jnp.minimum(first + chunks, last)])
    return jnp.concatenate(parts, axis=1)


def contract(a, b):
    return lax.dot_general(a, b, (((1,), (1,)), ((), ())), preferred_element_type=F32)


def value_kernel(off_ref, x_ref, p_ref, xr_ref, lo_ref, hi_ref, c_ref, stage, c32):
    k = pl.program_id(0)
    slots = pl.num_programs(0)
    cols, planes, ny, nz = x_ref.shape
    halves = nz // LANES
    chunks = p_ref.shape[2] // LANES
    per_plane = ny * halves

    @pl.when(k == 0)
    def _():
        for x in range(planes):
            for half in range(halves):
                piece = x_ref[:, x, :, half * LANES : (half + 1) * LANES].astype(F32)
                stage[half] = piece.reshape(cols * ny, LANES)
                for y in range(ny):
                    row = stage[half, pl.ds(y, cols, stride=ny), :].astype(BF)
                    h = (x * ny + y) * halves + half
                    xr_ref[h] = row
                    if x == 0:
                        lo_ref[h] = row
                    if x == planes - 1:
                        hi_ref[h - x * per_plane] = row

    off = off_ref[k]
    proj = shifted(p_ref, off & (LANES - 1), chunks)
    field = window_of(xr_ref, off >> 7, chunks)
    c32[pl.ds(pl.multiple_of(k * cols, cols), cols), :] = contract(field, proj)

    @pl.when(k == slots - 1)
    def _():
        dests = c_ref.shape[0]
        per = cols // dests
        for j in range(cols):
            row = c32[pl.ds(j, dests, stride=cols), :]
            c_ref[j // per, :, (j % per) * LANES : (j % per + 1) * LANES] = row.astype(BF)


def force_kernel(
    off_ref, blk_ref, brick_ref, w_ref, xr_ref, before_ref, after_ref, p_ref, c_ref, t_ref, fields, e32
):
    k = pl.program_id(0)
    slots = pl.num_programs(0)
    rows, cols, _ = xr_ref.shape
    per_plane = before_ref.shape[0]
    chunks = p_ref.shape[2] // LANES

    @pl.when(k == 0)
    def _():
        lane = lax.broadcasted_iota(jnp.int32, (cols, LANES), 1)

        def pair(r, carry):
            y_pair = r % (per_plane // 2)
            base = r - y_pair
            up = 2 * (base + (y_pair + 1) % (per_plane // 2))
            down = 2 * (base + (y_pair + per_plane // 2 - 1) % (per_plane // 2))
            h = 2 * r
            for half in range(2):
                fields[h + half, cols : 2 * cols] = xr_ref[up + half] - xr_ref[down + half]
            a = xr_ref[h]
            b = xr_ref[h + 1]
            a_up = pltpu.roll(a, LANES - 1, 1)
            b_up = pltpu.roll(b, LANES - 1, 1)
            a_down = pltpu.roll(a, 1, 1)
            b_down = pltpu.roll(b, 1, 1)
            last = lane == LANES - 1
            first = lane == 0
            fields[h, 2 * cols :] = jnp.where(last, b_up, a_up) - jnp.where(first, b_down, a_down)
            fields[h + 1, 2 * cols :] = jnp.where(last, a_up, b_up) - jnp.where(first, a_down, b_down)
            return carry

        lax.fori_loop(0, rows // 2, pair, 0)

        def inner(h, carry):
            fields[h, :cols] = xr_ref[h + per_plane] - xr_ref[h - per_plane]
            return carry

        lax.fori_loop(per_plane, rows - per_plane, inner, 0)

        def edge(h, carry):
            fields[h, :cols] = xr_ref[h + per_plane] - before_ref[h]
            t = rows - per_plane + h
            fields[t, :cols] = after_ref[h] - xr_ref[t - per_plane]
            return carry

        lax.fori_loop(0, per_plane, edge, 0)

    off = off_ref[k]
    proj = shifted(p_ref, off & (LANES - 1), chunks)
    field = window_of(fields, off >> 7, chunks)
    e32[pl.ds(pl.multiple_of(k * 3 * cols, 3 * cols), 3 * cols), :] = contract(field, proj)

    @pl.when(k == slots - 1)
    def _():
        n_slots = blk_ref.shape[1]
        per = cols // c_ref.shape[0]
        w = w_ref[0]
        sums = [jnp.zeros((n_slots, LANES), F32) for _ in range(3)]
        for j in range(cols):
            c = c_ref[j // per, :, (j % per) * LANES : (j % per + 1) * LANES].astype(F32)
            for x in range(3):
                sums[x] = sums[x] + c * e32[pl.ds(x * cols + j, n_slots, stride=3 * cols), :]
        t_ref[...] = jnp.zeros(t_ref.shape, F32)
        owned = t_ref.shape[1]
        brick = brick_ref[0]
        place = lax.broadcasted_iota(jnp.int32, (owned, 3 * LANES), 0)
        both = jnp.concatenate(sums, axis=1) * w
        for s in range(n_slots):
            g = blk_ref[brick, s]
            o = g // owned
            t_ref[o] = t_ref[o] + jnp.where(place == g % owned, both[s : s + 1], 0.0)


def owner_kernel(t_ref, coef_ref, atom_ref, out_ref):
    owned = coef_ref.shape[0]
    scale = -coef_ref[...]
    atom_id = lax.broadcasted_iota(jnp.int32, (LANES, LANES), 0)
    total = t_ref[0]
    for s in range(1, t_ref.shape[0]):
        total = total + t_ref[s]
    hits = [atom_ref[b : b + 1, :] == atom_id for b in range(owned)]
    row = lax.broadcasted_iota(jnp.int32, (8, LANES), 0)
    ones = jnp.ones((8, LANES), F32)
    out = jnp.zeros((8, LANES), F32)
    for x in range(3):
        terms = total[:, x * LANES : (x + 1) * LANES] * scale
        acc = jnp.zeros((LANES, LANES), F32)
        for b in range(owned):
            acc = acc + jnp.where(hits[b], terms[b : b + 1, :], 0.0)
        sums = lax.dot_general(
            ones, acc, (((1,), (1,)), ((), ())),
            preferred_element_type=F32, precision=lax.Precision.HIGHEST,
        )
        out = jnp.where(row == x, sums, out)
    for d in range(out_ref.shape[0]):
        out_ref[d] = out


def whole(shape):
    zeros = (0,) * len(shape)
    return pl.BlockSpec(shape, lambda k, *_: zeros)


def per_device(solution, proj_vals, slot_offset, slot_block, proj_coef, pole_weight, proj_atom):
    _, cols, planes, ny, nz = solution.shape
    slots, proj, win = proj_vals.shape
    bricks = lax.axis_size("grid")
    owned = proj_coef.shape[0]
    rows = planes * ny * nz // LANES
    per_plane = rows // planes
    per = cols // bricks
    brick = lax.axis_index("grid").astype(jnp.int32)
    x = solution.reshape(cols, planes, ny, nz)
    p_spec = pl.BlockSpec((1, proj, win), lambda k, *_: (k, 0, 0))

    xr, lo, hi, c_part = pl.pallas_call(
        value_kernel,
        out_shape=(
            jax.ShapeDtypeStruct((rows, cols, LANES), BF),
            jax.ShapeDtypeStruct((per_plane, cols, LANES), BF),
            jax.ShapeDtypeStruct((per_plane, cols, LANES), BF),
            jax.ShapeDtypeStruct((bricks, slots, per * LANES), BF),
        ),
        grid_spec=pltpu.PrefetchScalarGridSpec(
            num_scalar_prefetch=1,
            grid=(slots,),
            in_specs=[whole(x.shape), p_spec],
            out_specs=[
                whole((rows, cols, LANES)),
                whole((per_plane, cols, LANES)),
                whole((per_plane, cols, LANES)),
                whole((bricks, slots, per * LANES)),
            ],
            scratch_shapes=[
                pltpu.VMEM((nz // LANES, cols * ny, LANES), F32),
                pltpu.VMEM((slots * cols, LANES), F32),
            ],
        ),
        compiler_params=pltpu.CompilerParams(vmem_limit_bytes=48 << 20),
        name="values",
    )(slot_offset, x, proj_vals)

    up = [(i, (i + 1) % bricks) for i in range(bricks)]
    down = [(j, i) for i, j in up]
    before = lax.ppermute(hi, "grid", up)
    after = lax.ppermute(lo, "grid", down)

    arrived = lax.all_to_all(c_part, "grid", 0, 0, tiled=True)
    ids = slot_block.reshape(-1)
    same = (ids[:, None] == ids[None, :]).astype(BF)
    summed = jnp.dot(
        same, arrived.reshape(bricks * slots, per * LANES), preferred_element_type=F32
    ).astype(BF)
    coefs = lax.all_to_all(
        summed.reshape(bricks, slots, per * LANES), "grid", 0, 0, tiled=True
    )

    terms = pl.pallas_call(
        force_kernel,
        out_shape=jax.ShapeDtypeStruct((bricks, owned, 3 * LANES), F32),
        grid_spec=pltpu.PrefetchScalarGridSpec(
            num_scalar_prefetch=4,
            grid=(slots,),
            in_specs=[
                whole((rows, cols, LANES)),
                whole((per_plane, cols, LANES)),
                whole((per_plane, cols, LANES)),
                p_spec,
                whole((bricks, slots, per * LANES)),
            ],
            out_specs=whole((bricks, owned, 3 * LANES)),
            scratch_shapes=[
                pltpu.VMEM((rows, 3 * cols, LANES), BF),
                pltpu.VMEM((slots * 3 * cols, LANES), F32),
            ],
        ),
        compiler_params=pltpu.CompilerParams(vmem_limit_bytes=48 << 20),
        name="derivatives",
    )(slot_offset, slot_block, brick[None], pole_weight, xr, before, after, proj_vals, coefs)

    at_owner = lax.all_to_all(terms, "grid", 0, 0, tiled=True)
    copies = lax.axis_size("band") * lax.axis_size("pole")
    shares = pl.pallas_call(
        owner_kernel,
        out_shape=jax.ShapeDtypeStruct((copies, 8, LANES), F32),
        name="owner",
    )(at_owner, proj_coef, proj_atom)
    gathered = lax.all_to_all(shares, ("band", "pole"), 0, 0, tiled=True)
    return jnp.sum(gathered[:, :3, :ATOM_OWN], axis=0)


def solution(mesh):
    placed = (
        P("pole", "band", "grid", None, None),
        P("grid", None, None),
        P("grid"),
        P(),
        P("grid", None),
        P("pole"),
        P("grid", None),
    )
    return jax.shard_map(
        per_device, mesh=mesh, in_specs=placed, out_specs=P(None, "grid"), check_vma=False
    )
```

```python
import jax
import jax.numpy as jnp
from jax import lax
from jax.experimental import pallas as pl
from jax.experimental.pallas import tpu as pltpu
from jax.sharding import PartitionSpec as P

ATOM_OWN = 56
LANES = 128
BF = jnp.bfloat16
LIMIT = 57
NY = 16
GROUP = 8
VALUE_GROUP = 4
AHEAD = 8
GROUP_COLS = 16
F32 = jnp.float32


def shifted(block, shift, chunks):
    lane = lax.broadcasted_iota(jnp.int32, (block.shape[0], LANES), 1)
    low = lane < shift
    rolled = [
        pltpu.roll(block[:, j * LANES : (j + 1) * LANES], shift, 1) for j in range(chunks)
    ]
    zero = jnp.zeros_like(rolled[0])
    pieces = [jnp.where(low, zero, rolled[0])]
    for j in range(1, chunks):
        pieces.append(jnp.where(low, rolled[j - 1], rolled[j]))
    pieces.append(jnp.where(low, rolled[-1], zero))
    return jnp.concatenate(pieces, axis=1)


def window_of(field_ref, first, chunks):
    last = field_ref.shape[0] - 1
    parts = [field_ref[first + j] for j in range(chunks - 1)]
    parts.append(field_ref[jnp.minimum(first + chunks - 1, last)])
    return jnp.concatenate(parts, axis=1)


def contract(a, b):
    return lax.dot_general(a, b, (((1,), (1,)), ((), ())), preferred_element_type=F32)


def value_kernel(
    off_hbm, x_hbm, p_hbm, xr_hbm, lo_hbm, hi_hbm, c_ref, off, xbuf, pbuf, xr, stage, c32, osem, xsem, psem, rsem
):
    cols, planes, ny, nz = xbuf.shape
    slots = pbuf.shape[0]
    halves = nz // LANES
    chunks = pbuf.shape[2] // LANES
    per_plane = ny * halves

    def x_copy(g):
        part = pl.ds(g * GROUP_COLS, GROUP_COLS)
        return pltpu.make_async_copy(x_hbm.at[part], xbuf.at[part], xsem.at[g])

    def p_copy(k):
        return pltpu.make_async_copy(p_hbm.at[k], pbuf.at[k], psem.at[k])

    def plane(x):
        return pl.ds(x * per_plane, per_plane)

    for g in range(cols // GROUP_COLS):
        x_copy(g).start()
    off_copy = pltpu.make_async_copy(off_hbm, off, osem)
    off_copy.start()
    for k in range(AHEAD):
        p_copy(k).start()
    outgoing = [
        pltpu.make_async_copy(xr, xr_hbm, rsem.at[0]),
        pltpu.make_async_copy(xr.at[plane(0)], lo_hbm, rsem.at[1]),
        pltpu.make_async_copy(xr.at[plane(planes - 1)], hi_hbm, rsem.at[2]),
    ]
    for g in range(cols // GROUP_COLS):
        x_copy(g).wait()
        part = slice(g * GROUP_COLS, (g + 1) * GROUP_COLS)
        for x in range(planes):
            for half in range(halves):
                piece = xbuf[part, x, :, half * LANES : (half + 1) * LANES].astype(F32)
                stage[x, half] = piece.reshape(GROUP_COLS * ny, LANES)
                for y in range(ny):
                    row = stage[x, half, pl.ds(y, GROUP_COLS, stride=ny), :].astype(BF)
                    xr[(x * ny + y) * halves + half, part] = row
    for copy in outgoing:
        copy.start()
    off_copy.wait()

    def group(i, carry):
        for u in range(VALUE_GROUP):
            p_copy(i * VALUE_GROUP + u).wait()

        @pl.when(i * VALUE_GROUP + AHEAD < slots)
        def _():
            for u in range(VALUE_GROUP):
                p_copy(i * VALUE_GROUP + u + AHEAD).start()

        for u in range(VALUE_GROUP):
            k = i * VALUE_GROUP + u
            proj = shifted(pbuf[k], off[k] & (LANES - 1), chunks)
            field = window_of(xr, off[k] >> 7, chunks + 1)
            c32[pl.ds(pl.multiple_of(k * cols, cols), cols), :] = contract(field, proj)
        return carry

    lax.fori_loop(0, slots // VALUE_GROUP, group, 0)

    dests = c_ref.shape[0]
    per = cols // dests
    for j in range(cols):
        row = c32[pl.ds(j, dests, stride=cols), :]
        c_ref[j // per, :, (j % per) * LANES : (j % per + 1) * LANES] = row.astype(BF)
    for copy in outgoing:
        copy.wait()


def fetch_blocks(off_hbm, off, p_hbm, pbuf, osem, psem):
    copies = [
        pltpu.make_async_copy(p_hbm.at[k], pbuf.at[k], psem.at[k]) for k in range(AHEAD)
    ]
    offsets = pltpu.make_async_copy(off_hbm, off, osem)
    offsets.start()
    for copy in copies:
        copy.start()
    return offsets


def partials(off, p_hbm, pbuf, psem, fields, e_ref):
    slots, _, win = pbuf.shape
    chunks = win // LANES

    def p_copy(k):
        return pltpu.make_async_copy(p_hbm.at[k], pbuf.at[k], psem.at[k])

    def group(i, carry):
        for u in range(GROUP):
            p_copy(i * GROUP + u).wait()

        @pl.when(i * GROUP + AHEAD < slots)
        def _():
            for u in range(GROUP):
                p_copy(i * GROUP + u + AHEAD).start()

        for u in range(GROUP):
            k = i * GROUP + u
            proj = shifted(pbuf[k], off[k] & (LANES - 1), chunks)
            field = window_of(fields, off[k] >> 7, chunks + 1)
            e_ref[k] = contract(field, proj).astype(BF)
        return carry

    lax.fori_loop(0, slots // GROUP, group, 0)


def inside_kernel(off_hbm, xr_hbm, p_hbm, e_ref, off, xr, fields, pbuf, osem, xsem, psem):
    rows, cols, _ = xr.shape
    xr_copy = pltpu.make_async_copy(xr_hbm, xr, xsem)
    xr_copy.start()
    offsets = fetch_blocks(off_hbm, off, p_hbm, pbuf, osem, psem)
    lane = lax.broadcasted_iota(jnp.int32, (cols, LANES), 1)
    last = lane == LANES - 1
    first = lane == 0

    def pair(r, carry):
        y = r % NY
        up = 2 * (r - y + (y + 1) % NY)
        down = 2 * (r - y + (y + NY - 1) % NY)
        h = 2 * r
        for half in range(2):
            fields[h + half, :cols] = xr[up + half] - xr[down + half]
        a = xr[h]
        b = xr[h + 1]
        a_up = pltpu.roll(a, LANES - 1, 1)
        b_up = pltpu.roll(b, LANES - 1, 1)
        a_down = pltpu.roll(a, 1, 1)
        b_down = pltpu.roll(b, 1, 1)
        fields[h, cols:] = jnp.where(last, b_up, a_up) - jnp.where(first, b_down, a_down)
        fields[h + 1, cols:] = jnp.where(last, a_up, b_up) - jnp.where(first, a_down, b_down)
        return carry

    xr_copy.wait()
    lax.fori_loop(0, rows // 2, pair, 0, unroll=4)
    offsets.wait()
    partials(off, p_hbm, pbuf, psem, fields, e_ref)


def across_kernel(
    off_hbm, xr_hbm, before_ref, after_ref, p_hbm, e_ref, off, xr, fields, pbuf, osem, xsem, psem
):
    rows = xr.shape[0]
    per_plane = before_ref.shape[0]
    xr_copy = pltpu.make_async_copy(xr_hbm, xr, xsem)
    xr_copy.start()
    offsets = fetch_blocks(off_hbm, off, p_hbm, pbuf, osem, psem)

    def inner(h, carry):
        fields[h] = xr[h + per_plane] - xr[h - per_plane]
        return carry

    def edge(h, carry):
        fields[h] = xr[h + per_plane] - before_ref[h]
        t = rows - per_plane + h
        fields[t] = after_ref[h] - xr[t - per_plane]
        return carry

    xr_copy.wait()
    lax.fori_loop(per_plane, rows - per_plane, inner, 0, unroll=8)
    lax.fori_loop(0, per_plane, edge, 0, unroll=8)
    offsets.wait()
    partials(off, p_hbm, pbuf, psem, fields, e_ref)


def term_kernel(blk_ref, brick_ref, w_ref, c_ref, ex_ref, eyz_ref, t_ref, c32):
    dests, slots, _ = c_ref.shape
    cols = ex_ref.shape[1]
    per = cols // dests
    for j in range(cols):
        c = c_ref[j // per, :, (j % per) * LANES : (j % per + 1) * LANES].astype(F32)
        c32[pl.ds(j, slots, stride=cols), :] = c
    t_ref[...] = jnp.zeros(t_ref.shape, F32)
    owned = t_ref.shape[1]
    brick = brick_ref[0]
    w = w_ref[0]
    place = lax.broadcasted_iota(jnp.int32, (owned, LANES), 0)
    for k in range(slots):
        c = c32[k * cols : (k + 1) * cols] * w
        g = blk_ref[brick, k]
        o = g // owned
        here = place == g % owned
        parts = (ex_ref[k], eyz_ref[k, :cols], eyz_ref[k, cols:])
        for x in range(3):
            term = jnp.sum(c * parts[x].astype(F32), axis=0, keepdims=True)
            at = slice(x * LANES, (x + 1) * LANES)
            t_ref[o, :, at] = t_ref[o, :, at] + jnp.where(here, term, 0.0)


def owner_kernel(t_ref, coef_ref, atom_ref, out_ref):
    owned = coef_ref.shape[0]
    scale = -coef_ref[...]
    atom_id = lax.broadcasted_iota(jnp.int32, (LANES, LANES), 0)
    total = t_ref[0]
    for s in range(1, t_ref.shape[0]):
        total = total + t_ref[s]
    hits = [atom_ref[b : b + 1, :] == atom_id for b in range(owned)]
    row = lax.broadcasted_iota(jnp.int32, (8, LANES), 0)
    ones = jnp.ones((8, LANES), F32)
    out = jnp.zeros((8, LANES), F32)
    for x in range(3):
        terms = total[:, x * LANES : (x + 1) * LANES] * scale
        acc = jnp.zeros((LANES, LANES), F32)
        for b in range(owned):
            acc = acc + jnp.where(hits[b], terms[b : b + 1, :], 0.0)
        sums = lax.dot_general(
            ones, acc, (((1,), (1,)), ((), ())),
            preferred_element_type=F32, precision=lax.Precision.HIGHEST,
        )
        out = jnp.where(row == x, sums, out)
    for d in range(out_ref.shape[0]):
        out_ref[d] = out


def forces(solution, proj_vals, slot_offset, slot_block, proj_coef, pole_weight, proj_atom):
    _, cols, planes, ny, nz = solution.shape
    slots, proj, win = proj_vals.shape
    bricks = lax.axis_size("grid")
    owned = proj_coef.shape[0]
    rows = planes * ny * nz // LANES
    per_plane = rows // planes
    per = cols // bricks
    brick = lax.axis_index("grid").astype(jnp.int32)
    x = solution.reshape(cols, planes, ny, nz)

    def params(mib):
        return pltpu.CompilerParams(vmem_limit_bytes=mib << 20)

    smem = pl.BlockSpec(memory_space=pltpu.SMEM)
    vmem = pl.BlockSpec(memory_space=pltpu.VMEM)
    hbm = pl.BlockSpec(memory_space=pltpu.HBM)

    dma = pltpu.SemaphoreType.DMA
    xr, lo, hi, c_part = pl.pallas_call(
        value_kernel,
        out_shape=(
            jax.ShapeDtypeStruct((rows, cols, LANES), BF),
            jax.ShapeDtypeStruct((per_plane, cols, LANES), BF),
            jax.ShapeDtypeStruct((per_plane, cols, LANES), BF),
            jax.ShapeDtypeStruct((bricks, slots, per * LANES), BF),
        ),
        in_specs=[hbm, hbm, hbm],
        out_specs=[hbm, hbm, hbm, vmem],
        scratch_shapes=[
            pltpu.SMEM((slots,), jnp.int32),
            pltpu.VMEM((cols, planes, ny, nz), BF),
            pltpu.VMEM((slots, proj, win), BF),
            pltpu.VMEM((rows, cols, LANES), BF),
            pltpu.VMEM((planes, nz // LANES, GROUP_COLS * ny, LANES), F32),
            pltpu.VMEM((slots * cols, LANES), F32),
            dma,
            dma((cols // GROUP_COLS,)),
            dma((slots,)),
            dma((3,)),
        ],
        compiler_params=params(LIMIT),
        name="values",
    )(slot_offset, x, proj_vals)

    arrived = lax.all_to_all(c_part, "grid", 0, 0, tiled=True)

    up = [(i, (i + 1) % bricks) for i in range(bricks)]
    down = [(j, i) for i, j in up]
    before = lax.ppermute(hi, "grid", up)
    after = lax.ppermute(lo, "grid", down)

    def scratch(fields):
        return [
            pltpu.SMEM((slots,), jnp.int32),
            pltpu.VMEM((rows, cols, LANES), BF),
            pltpu.VMEM((rows, fields * cols, LANES), BF),
            pltpu.VMEM((slots, proj, win), BF),
            dma,
            dma,
            dma((slots,)),
        ]

    e_yz = pl.pallas_call(
        inside_kernel,
        out_shape=jax.ShapeDtypeStruct((slots, 2 * cols, LANES), BF),
        in_specs=[hbm] * 3,
        out_specs=vmem,
        scratch_shapes=scratch(2),
        compiler_params=params(LIMIT),
        name="inside",
    )(slot_offset, xr, proj_vals)

    arrived, e_yz = lax.optimization_barrier((arrived, e_yz))
    ids = slot_block.reshape(-1)
    same = (ids[:, None] == ids[None, :]).astype(BF)
    summed = jnp.dot(
        same, arrived.reshape(bricks * slots, per * LANES), preferred_element_type=F32
    ).astype(BF)
    coefs = lax.all_to_all(
        summed.reshape(bricks, slots, per * LANES), "grid", 0, 0, tiled=True
    )

    e_x = pl.pallas_call(
        across_kernel,
        out_shape=jax.ShapeDtypeStruct((slots, cols, LANES), BF),
        in_specs=[hbm, hbm, vmem, vmem, hbm],
        out_specs=vmem,
        scratch_shapes=scratch(1),
        compiler_params=params(LIMIT),
        name="across",
    )(slot_offset, xr, before, after, proj_vals)

    terms = pl.pallas_call(
        term_kernel,
        out_shape=jax.ShapeDtypeStruct((bricks, owned, 3 * LANES), F32),
        in_specs=[smem, smem, smem, vmem, vmem, vmem],
        out_specs=vmem,
        scratch_shapes=[pltpu.VMEM((slots * cols, LANES), F32)],
        compiler_params=params(8),
        name="terms",
    )(slot_block, brick[None], pole_weight, coefs, e_x, e_yz)

    at_owner = lax.all_to_all(terms, "grid", 0, 0, tiled=True)
    copies = lax.axis_size("band") * lax.axis_size("pole")
    shares = pl.pallas_call(
        owner_kernel,
        out_shape=jax.ShapeDtypeStruct((copies, 8, LANES), F32),
        name="owner",
    )(at_owner, proj_coef, proj_atom)
    gathered = lax.all_to_all(shares, ("band", "pole"), 0, 0, tiled=True)
    return jnp.sum(gathered[:, :3, :ATOM_OWN], axis=0)


def solution(mesh):
    placed = (
        P("pole", "band", "grid", None, None),
        P("grid", None, None),
        P("grid"),
        P(),
        P("grid", None),
        P("pole"),
        P("grid", None),
    )
    return jax.shard_map(
        forces, mesh=mesh, in_specs=placed, out_specs=P(None, "grid"), check_vma=False
    )
```

```python
import jax
import jax.numpy as jnp
from jax import lax
from jax.experimental import pallas as pl
from jax.experimental.pallas import tpu as pltpu
from jax.sharding import PartitionSpec as P

ATOM_OWN = 56
LANES = 128
BF = jnp.bfloat16
LIMIT = 24
NY = 16
GROUP = 8
VALUE_GROUP = 4
AHEAD = 8
GROUP_COLS = 16
F32 = jnp.float32


def shifted(block, shift, chunks):
    lane = lax.broadcasted_iota(jnp.int32, (block.shape[0], LANES), 1)
    low = lane < shift
    rolled = [
        pltpu.roll(block[:, j * LANES : (j + 1) * LANES], shift, 1) for j in range(chunks)
    ]
    zero = jnp.zeros_like(rolled[0])
    pieces = [jnp.where(low, zero, rolled[0])]
    for j in range(1, chunks):
        pieces.append(jnp.where(low, rolled[j - 1], rolled[j]))
    pieces.append(jnp.where(low, rolled[-1], zero))
    return jnp.concatenate(pieces, axis=1)


def window_of(field_ref, first, chunks):
    last = field_ref.shape[0] - 1
    parts = [field_ref[first + j] for j in range(chunks - 1)]
    parts.append(field_ref[jnp.minimum(first + chunks - 1, last)])
    return jnp.concatenate(parts, axis=1)


def contract(a, b):
    return lax.dot_general(a, b, (((1,), (1,)), ((), ())), preferred_element_type=F32)


def value_kernel(
    off_hbm, x_hbm, p_hbm, xr_hbm, lo_hbm, hi_hbm, c_ref, off, xbuf, pbuf, xr, stage, c32, osem, xsem, psem, rsem
):
    cols, planes, ny, nz = xbuf.shape
    slots = pbuf.shape[0]
    halves = nz // LANES
    chunks = pbuf.shape[2] // LANES
    per_plane = ny * halves

    def x_copy(g):
        part = pl.ds(g * GROUP_COLS, GROUP_COLS)
        return pltpu.make_async_copy(x_hbm.at[part], xbuf.at[part], xsem.at[g])

    def p_copy(k):
        return pltpu.make_async_copy(p_hbm.at[k], pbuf.at[k], psem.at[k])

    def plane(x):
        return pl.ds(x * per_plane, per_plane)

    for g in range(cols // GROUP_COLS):
        x_copy(g).start()
    off_copy = pltpu.make_async_copy(off_hbm, off, osem)
    off_copy.start()
    for k in range(AHEAD):
        p_copy(k).start()
    outgoing = [
        pltpu.make_async_copy(xr, xr_hbm, rsem.at[0]),
        pltpu.make_async_copy(xr.at[plane(0)], lo_hbm, rsem.at[1]),
        pltpu.make_async_copy(xr.at[plane(planes - 1)], hi_hbm, rsem.at[2]),
    ]
    for g in range(cols // GROUP_COLS):
        x_copy(g).wait()
        part = slice(g * GROUP_COLS, (g + 1) * GROUP_COLS)
        for x in range(planes):
            for half in range(halves):
                piece = xbuf[part, x, :, half * LANES : (half + 1) * LANES].astype(F32)
                stage[x, half] = piece.reshape(GROUP_COLS * ny, LANES)
                for y in range(ny):
                    row = stage[x, half, pl.ds(y, GROUP_COLS, stride=ny), :].astype(BF)
                    xr[(x * ny + y) * halves + half, part] = row
    for copy in outgoing:
        copy.start()
    off_copy.wait()

    def group(i, carry):
        for u in range(VALUE_GROUP):
            p_copy(i * VALUE_GROUP + u).wait()

        @pl.when(i * VALUE_GROUP + AHEAD < slots)
        def _():
            for u in range(VALUE_GROUP):
                p_copy(i * VALUE_GROUP + u + AHEAD).start()

        for u in range(VALUE_GROUP):
            k = i * VALUE_GROUP + u
            proj = shifted(pbuf[k], off[k] & (LANES - 1), chunks)
            field = window_of(xr, off[k] >> 7, chunks + 1)
            c32[pl.ds(pl.multiple_of(k * cols, cols), cols), :] = contract(field, proj)
        return carry

    lax.fori_loop(0, slots // VALUE_GROUP, group, 0)

    dests = c_ref.shape[0]
    per = cols // dests
    for j in range(cols):
        row = c32[pl.ds(j, dests, stride=cols), :]
        c_ref[j // per, :, (j % per) * LANES : (j % per + 1) * LANES] = row.astype(BF)
    for copy in outgoing:
        copy.wait()


def fetch_blocks(off_hbm, off, p_hbm, pbuf, osem, psem):
    copies = [
        pltpu.make_async_copy(p_hbm.at[k], pbuf.at[k], psem.at[k]) for k in range(AHEAD)
    ]
    offsets = pltpu.make_async_copy(off_hbm, off, osem)
    offsets.start()
    for copy in copies:
        copy.start()
    return offsets


def partials(off, p_hbm, pbuf, psem, fields, e_ref):
    slots, _, win = pbuf.shape
    chunks = win // LANES

    def p_copy(k):
        return pltpu.make_async_copy(p_hbm.at[k], pbuf.at[k], psem.at[k])

    def group(i, carry):
        for u in range(GROUP):
            p_copy(i * GROUP + u).wait()

        @pl.when(i * GROUP + AHEAD < slots)
        def _():
            for u in range(GROUP):
                p_copy(i * GROUP + u + AHEAD).start()

        for u in range(GROUP):
            k = i * GROUP + u
            proj = shifted(pbuf[k], off[k] & (LANES - 1), chunks)
            field = window_of(fields, off[k] >> 7, chunks + 1)
            e_ref[k] = contract(field, proj).astype(BF)
        return carry

    lax.fori_loop(0, slots // GROUP, group, 0)


def inside_kernel(off_hbm, xr_hbm, p_hbm, e_ref, off, xr, fields, pbuf, osem, xsem, psem):
    rows, cols, _ = xr.shape
    xr_copy = pltpu.make_async_copy(xr_hbm, xr, xsem)
    xr_copy.start()
    offsets = fetch_blocks(off_hbm, off, p_hbm, pbuf, osem, psem)
    lane = lax.broadcasted_iota(jnp.int32, (cols, LANES), 1)
    last = lane == LANES - 1
    first = lane == 0

    def pair(r, carry):
        y = r % NY
        up = 2 * (r - y + (y + 1) % NY)
        down = 2 * (r - y + (y + NY - 1) % NY)
        h = 2 * r
        for half in range(2):
            fields[h + half, :cols] = xr[up + half] - xr[down + half]
        a = xr[h]
        b = xr[h + 1]
        a_up = pltpu.roll(a, LANES - 1, 1)
        b_up = pltpu.roll(b, LANES - 1, 1)
        a_down = pltpu.roll(a, 1, 1)
        b_down = pltpu.roll(b, 1, 1)
        fields[h, cols:] = jnp.where(last, b_up, a_up) - jnp.where(first, b_down, a_down)
        fields[h + 1, cols:] = jnp.where(last, a_up, b_up) - jnp.where(first, a_down, b_down)
        return carry

    xr_copy.wait()
    lax.fori_loop(0, rows // 2, pair, 0, unroll=4)
    offsets.wait()
    partials(off, p_hbm, pbuf, psem, fields, e_ref)


def across_kernel(
    off_hbm, xr_hbm, before_ref, after_ref, p_hbm, e_ref, off, xr, fields, pbuf, osem, xsem, psem
):
    rows = xr.shape[0]
    per_plane = before_ref.shape[0]
    xr_copy = pltpu.make_async_copy(xr_hbm, xr, xsem)
    xr_copy.start()
    offsets = fetch_blocks(off_hbm, off, p_hbm, pbuf, osem, psem)

    def inner(h, carry):
        fields[h] = xr[h + per_plane] - xr[h - per_plane]
        return carry

    def edge(h, carry):
        fields[h] = xr[h + per_plane] - before_ref[h]
        t = rows - per_plane + h
        fields[t] = after_ref[h] - xr[t - per_plane]
        return carry

    xr_copy.wait()
    lax.fori_loop(per_plane, rows - per_plane, inner, 0, unroll=8)
    lax.fori_loop(0, per_plane, edge, 0, unroll=8)
    offsets.wait()
    partials(off, p_hbm, pbuf, psem, fields, e_ref)


def term_kernel(blk_ref, brick_ref, w_ref, c_ref, ex_ref, eyz_ref, t_ref, c32):
    dests, slots, _ = c_ref.shape
    cols = ex_ref.shape[1]
    per = cols // dests
    for j in range(cols):
        c = c_ref[j // per, :, (j % per) * LANES : (j % per + 1) * LANES].astype(F32)
        c32[pl.ds(j, slots, stride=cols), :] = c
    t_ref[...] = jnp.zeros(t_ref.shape, F32)
    owned = t_ref.shape[1]
    brick = brick_ref[0]
    w = w_ref[0]
    place = lax.broadcasted_iota(jnp.int32, (owned, LANES), 0)
    for k in range(slots):
        c = c32[k * cols : (k + 1) * cols] * w
        g = blk_ref[brick, k]
        o = g // owned
        here = place == g % owned
        parts = (ex_ref[k], eyz_ref[k, :cols], eyz_ref[k, cols:])
        for x in range(3):
            term = jnp.sum(c * parts[x].astype(F32), axis=0, keepdims=True)
            at = slice(x * LANES, (x + 1) * LANES)
            t_ref[o, :, at] = t_ref[o, :, at] + jnp.where(here, term, 0.0)


def owner_kernel(t_ref, coef_ref, atom_ref, out_ref):
    owned = coef_ref.shape[0]
    scale = -coef_ref[...]
    atom_id = lax.broadcasted_iota(jnp.int32, (LANES, LANES), 0)
    total = t_ref[0]
    for s in range(1, t_ref.shape[0]):
        total = total + t_ref[s]
    hits = [atom_ref[b : b + 1, :] == atom_id for b in range(owned)]
    row = lax.broadcasted_iota(jnp.int32, (8, LANES), 0)
    ones = jnp.ones((8, LANES), F32)
    out = jnp.zeros((8, LANES), F32)
    for x in range(3):
        terms = total[:, x * LANES : (x + 1) * LANES] * scale
        acc = jnp.zeros((LANES, LANES), F32)
        for b in range(owned):
            acc = acc + jnp.where(hits[b], terms[b : b + 1, :], 0.0)
        sums = lax.dot_general(
            ones, acc, (((1,), (1,)), ((), ())),
            preferred_element_type=F32, precision=lax.Precision.HIGHEST,
        )
        out = jnp.where(row == x, sums, out)
    for d in range(out_ref.shape[0]):
        out_ref[d] = out


def forces(solution, proj_vals, slot_offset, slot_block, proj_coef, pole_weight, proj_atom):
    _, cols, planes, ny, nz = solution.shape
    slots, proj, win = proj_vals.shape
    bricks = lax.axis_size("grid")
    owned = proj_coef.shape[0]
    rows = planes * ny * nz // LANES
    per_plane = rows // planes
    per = cols // bricks
    brick = lax.axis_index("grid").astype(jnp.int32)
    x = pltpu.with_memory_space_constraint(solution.reshape(cols, planes, ny, nz), pltpu.HBM)
    proj_vals = pltpu.with_memory_space_constraint(proj_vals, pltpu.HBM)
    slot_offset = pltpu.with_memory_space_constraint(slot_offset, pltpu.HBM)

    def params(mib):
        return pltpu.CompilerParams(vmem_limit_bytes=mib << 20)

    smem = pl.BlockSpec(memory_space=pltpu.SMEM)
    vmem = pl.BlockSpec(memory_space=pltpu.VMEM)
    hbm = pl.BlockSpec(memory_space=pltpu.HBM)

    dma = pltpu.SemaphoreType.DMA
    xr, lo, hi, c_part = pl.pallas_call(
        value_kernel,
        out_shape=(
            jax.ShapeDtypeStruct((rows, cols, LANES), BF),
            jax.ShapeDtypeStruct((per_plane, cols, LANES), BF),
            jax.ShapeDtypeStruct((per_plane, cols, LANES), BF),
            jax.ShapeDtypeStruct((bricks, slots, per * LANES), BF),
        ),
        in_specs=[hbm, hbm, hbm],
        out_specs=[hbm, hbm, hbm, vmem],
        scratch_shapes=[
            pltpu.SMEM((slots,), jnp.int32),
            pltpu.VMEM((cols, planes, ny, nz), BF),
            pltpu.VMEM((slots, proj, win), BF),
            pltpu.VMEM((rows, cols, LANES), BF),
            pltpu.VMEM((planes, nz // LANES, GROUP_COLS * ny, LANES), F32),
            pltpu.VMEM((slots * cols, LANES), F32),
            dma,
            dma((cols // GROUP_COLS,)),
            dma((slots,)),
            dma((3,)),
        ],
        compiler_params=params(LIMIT),
        name="values",
    )(slot_offset, x, proj_vals)

    arrived = lax.all_to_all(c_part, "grid", 0, 0, tiled=True)

    up = [(i, (i + 1) % bricks) for i in range(bricks)]
    down = [(j, i) for i, j in up]
    before = lax.ppermute(hi, "grid", up)
    after = lax.ppermute(lo, "grid", down)

    def scratch(fields):
        return [
            pltpu.SMEM((slots,), jnp.int32),
            pltpu.VMEM((rows, cols, LANES), BF),
            pltpu.VMEM((rows, fields * cols, LANES), BF),
            pltpu.VMEM((slots, proj, win), BF),
            dma,
            dma,
            dma((slots,)),
        ]

    e_yz = pl.pallas_call(
        inside_kernel,
        out_shape=jax.ShapeDtypeStruct((slots, 2 * cols, LANES), BF),
        in_specs=[hbm] * 3,
        out_specs=vmem,
        scratch_shapes=scratch(2),
        compiler_params=params(LIMIT),
        name="inside",
    )(slot_offset, xr, proj_vals)

    arrived, e_yz = lax.optimization_barrier((arrived, e_yz))
    ids = slot_block.reshape(-1)
    same = (ids[:, None] == ids[None, :]).astype(BF)
    summed = jnp.dot(
        same, arrived.reshape(bricks * slots, per * LANES), preferred_element_type=F32
    ).astype(BF)
    coefs = lax.all_to_all(
        summed.reshape(bricks, slots, per * LANES), "grid", 0, 0, tiled=True
    )

    e_x = pl.pallas_call(
        across_kernel,
        out_shape=jax.ShapeDtypeStruct((slots, cols, LANES), BF),
        in_specs=[hbm, hbm, vmem, vmem, hbm],
        out_specs=vmem,
        scratch_shapes=scratch(1),
        compiler_params=params(LIMIT),
        name="across",
    )(slot_offset, xr, before, after, proj_vals)

    terms = pl.pallas_call(
        term_kernel,
        out_shape=jax.ShapeDtypeStruct((bricks, owned, 3 * LANES), F32),
        in_specs=[smem, smem, smem, vmem, vmem, vmem],
        out_specs=vmem,
        scratch_shapes=[pltpu.VMEM((slots * cols, LANES), F32)],
        compiler_params=params(8),
        name="terms",
    )(slot_block, brick[None], pole_weight, coefs, e_x, e_yz)

    at_owner = lax.all_to_all(terms, "grid", 0, 0, tiled=True)
    copies = lax.axis_size("band") * lax.axis_size("pole")
    shares = pl.pallas_call(
        owner_kernel,
        out_shape=jax.ShapeDtypeStruct((copies, 8, LANES), F32),
        name="owner",
    )(at_owner, proj_coef, proj_atom)
    gathered = lax.all_to_all(shares, ("band", "pole"), 0, 0, tiled=True)
    return jnp.sum(gathered[:, :3, :ATOM_OWN], axis=0)


def solution(mesh):
    placed = (
        P("pole", "band", "grid", None, None),
        P("grid", None, None),
        P("grid"),
        P(),
        P("grid", None),
        P("pole"),
        P("grid", None),
    )
    return jax.shard_map(
        forces, mesh=mesh, in_specs=placed, out_specs=P(None, "grid"), check_vma=False
    )
```

```python
import jax
import jax.numpy as jnp
from jax import lax
from jax.experimental import pallas as pl
from jax.experimental.pallas import tpu as pltpu
from jax.sharding import PartitionSpec as P

ATOM_OWN = 56
LANES = 128
BF = jnp.bfloat16
LIMIT = 24
NY = 16
GROUP = 4
VALUE_GROUP = 4
AHEAD = 8
GROUP_COLS = 16
F32 = jnp.float32


def shifted(block, shift, chunks):
    lane = lax.broadcasted_iota(jnp.int32, (block.shape[0], LANES), 1)
    low = lane < shift
    rolled = [
        pltpu.roll(block[:, j * LANES : (j + 1) * LANES], shift, 1) for j in range(chunks)
    ]
    zero = jnp.zeros_like(rolled[0])
    pieces = [jnp.where(low, zero, rolled[0])]
    for j in range(1, chunks):
        pieces.append(jnp.where(low, rolled[j - 1], rolled[j]))
    pieces.append(jnp.where(low, rolled[-1], zero))
    return jnp.concatenate(pieces, axis=1)


def window_of(field_ref, first, chunks):
    last = field_ref.shape[0] - 1
    parts = [field_ref[first + j] for j in range(chunks - 1)]
    parts.append(field_ref[jnp.minimum(first + chunks - 1, last)])
    return jnp.concatenate(parts, axis=1)


def contract(a, b):
    return lax.dot_general(a, b, (((1,), (1,)), ((), ())), preferred_element_type=F32)


def value_kernel(
    off_hbm, x_hbm, p_hbm, xr_hbm, lo_hbm, hi_hbm, c_ref, off, xbuf, pbuf, xr, stage, c32, osem, xsem, psem, rsem
):
    cols, planes, ny, nz = xbuf.shape
    slots = pbuf.shape[0]
    halves = nz // LANES
    chunks = pbuf.shape[2] // LANES
    per_plane = ny * halves

    def x_copy(g):
        part = pl.ds(g * GROUP_COLS, GROUP_COLS)
        return pltpu.make_async_copy(x_hbm.at[part], xbuf.at[part], xsem.at[g])

    def p_copy(k):
        return pltpu.make_async_copy(p_hbm.at[k], pbuf.at[k], psem.at[k])

    def plane(x):
        return pl.ds(x * per_plane, per_plane)

    for g in range(cols // GROUP_COLS):
        x_copy(g).start()
    off_copy = pltpu.make_async_copy(off_hbm, off, osem)
    off_copy.start()
    for k in range(AHEAD):
        p_copy(k).start()
    outgoing = [
        pltpu.make_async_copy(xr, xr_hbm, rsem.at[0]),
        pltpu.make_async_copy(xr.at[plane(0)], lo_hbm, rsem.at[1]),
        pltpu.make_async_copy(xr.at[plane(planes - 1)], hi_hbm, rsem.at[2]),
    ]
    for g in range(cols // GROUP_COLS):
        x_copy(g).wait()
        part = slice(g * GROUP_COLS, (g + 1) * GROUP_COLS)
        for x in range(planes):
            for half in range(halves):
                piece = xbuf[part, x, :, half * LANES : (half + 1) * LANES].astype(F32)
                stage[x, half] = piece.reshape(GROUP_COLS * ny, LANES)
                for y in range(ny):
                    row = stage[x, half, pl.ds(y, GROUP_COLS, stride=ny), :].astype(BF)
                    xr[(x * ny + y) * halves + half, part] = row
    for copy in outgoing:
        copy.start()
    off_copy.wait()

    def group(i, carry):
        for u in range(VALUE_GROUP):
            p_copy(i * VALUE_GROUP + u).wait()

        @pl.when(i * VALUE_GROUP + AHEAD < slots)
        def _():
            for u in range(VALUE_GROUP):
                p_copy(i * VALUE_GROUP + u + AHEAD).start()

        for u in range(VALUE_GROUP):
            k = i * VALUE_GROUP + u
            proj = shifted(pbuf[k], off[k] & (LANES - 1), chunks)
            field = window_of(xr, off[k] >> 7, chunks + 1)
            c32[pl.ds(pl.multiple_of(k * cols, cols), cols), :] = contract(field, proj)
        return carry

    lax.fori_loop(0, slots // VALUE_GROUP, group, 0)

    dests = c_ref.shape[0]
    per = cols // dests
    for j in range(cols):
        row = c32[pl.ds(j, dests, stride=cols), :]
        c_ref[j // per, :, (j % per) * LANES : (j % per + 1) * LANES] = row.astype(BF)
    for copy in outgoing:
        copy.wait()


def fetch_blocks(off_hbm, off, p_hbm, pbuf, osem, psem):
    copies = [
        pltpu.make_async_copy(p_hbm.at[k], pbuf.at[k], psem.at[k]) for k in range(AHEAD)
    ]
    offsets = pltpu.make_async_copy(off_hbm, off, osem)
    offsets.start()
    for copy in copies:
        copy.start()
    return offsets


def partials(off, p_hbm, pbuf, psem, fields, e_ref):
    slots, _, win = pbuf.shape
    chunks = win // LANES

    def p_copy(k):
        return pltpu.make_async_copy(p_hbm.at[k], pbuf.at[k], psem.at[k])

    def group(i, carry):
        for u in range(GROUP):
            p_copy(i * GROUP + u).wait()

        @pl.when(i * GROUP + AHEAD < slots)
        def _():
            for u in range(GROUP):
                p_copy(i * GROUP + u + AHEAD).start()

        for u in range(GROUP):
            k = i * GROUP + u
            proj = shifted(pbuf[k], off[k] & (LANES - 1), chunks)
            field = window_of(fields, off[k] >> 7, chunks + 1)
            e_ref[k] = contract(field, proj).astype(BF)
        return carry

    lax.fori_loop(0, slots // GROUP, group, 0)


def inside_kernel(off_hbm, xr_hbm, p_hbm, e_ref, off, xr, fields, pbuf, osem, xsem, psem):
    rows, cols, _ = xr.shape
    xr_copy = pltpu.make_async_copy(xr_hbm, xr, xsem)
    xr_copy.start()
    offsets = fetch_blocks(off_hbm, off, p_hbm, pbuf, osem, psem)
    lane = lax.broadcasted_iota(jnp.int32, (cols, LANES), 1)
    last = lane == LANES - 1
    first = lane == 0

    def pair(r, carry):
        y = r % NY
        up = 2 * (r - y + (y + 1) % NY)
        down = 2 * (r - y + (y + NY - 1) % NY)
        h = 2 * r
        for half in range(2):
            fields[h + half, :cols] = xr[up + half] - xr[down + half]
        a = xr[h]
        b = xr[h + 1]
        a_up = pltpu.roll(a, LANES - 1, 1)
        b_up = pltpu.roll(b, LANES - 1, 1)
        a_down = pltpu.roll(a, 1, 1)
        b_down = pltpu.roll(b, 1, 1)
        fields[h, cols:] = jnp.where(last, b_up, a_up) - jnp.where(first, b_down, a_down)
        fields[h + 1, cols:] = jnp.where(last, a_up, b_up) - jnp.where(first, a_down, b_down)
        return carry

    xr_copy.wait()
    lax.fori_loop(0, rows // 2, pair, 0, unroll=4)
    offsets.wait()
    partials(off, p_hbm, pbuf, psem, fields, e_ref)


def across_kernel(
    off_hbm, xr_hbm, before_ref, after_ref, p_hbm, e_ref, off, xr, fields, pbuf, osem, xsem, psem
):
    rows = xr.shape[0]
    per_plane = before_ref.shape[0]
    xr_copy = pltpu.make_async_copy(xr_hbm, xr, xsem)
    xr_copy.start()
    offsets = fetch_blocks(off_hbm, off, p_hbm, pbuf, osem, psem)

    def inner(h, carry):
        fields[h] = xr[h + per_plane] - xr[h - per_plane]
        return carry

    def edge(h, carry):
        fields[h] = xr[h + per_plane] - before_ref[h]
        t = rows - per_plane + h
        fields[t] = after_ref[h] - xr[t - per_plane]
        return carry

    xr_copy.wait()
    lax.fori_loop(per_plane, rows - per_plane, inner, 0, unroll=8)
    lax.fori_loop(0, per_plane, edge, 0, unroll=8)
    offsets.wait()
    partials(off, p_hbm, pbuf, psem, fields, e_ref)


def term_kernel(blk_ref, brick_ref, w_ref, c_ref, ex_ref, eyz_ref, out_ref, c32, t_ref):
    dests, slots, _ = c_ref.shape
    cols = ex_ref.shape[1]
    per = cols // dests
    for j in range(cols):
        c = c_ref[j // per, :, (j % per) * LANES : (j % per + 1) * LANES].astype(F32)
        c32[pl.ds(j, slots, stride=cols), :] = c
    t_ref[...] = jnp.zeros(t_ref.shape, F32)
    owned = t_ref.shape[1]
    brick = brick_ref[0]
    w = w_ref[0]
    place = lax.broadcasted_iota(jnp.int32, (owned, LANES), 0)
    for k in range(slots):
        c = c32[k * cols : (k + 1) * cols] * w
        g = blk_ref[brick, k]
        o = g // owned
        here = place == g % owned
        parts = (ex_ref[k], eyz_ref[k, :cols], eyz_ref[k, cols:])
        for x in range(3):
            term = jnp.sum(c * parts[x].astype(F32), axis=0, keepdims=True)
            at = slice(x * LANES, (x + 1) * LANES)
            t_ref[o, :, at] = t_ref[o, :, at] + jnp.where(here, term, 0.0)
    out_ref[...] = t_ref[...].astype(BF)


def owner_kernel(t_ref, coef_ref, atom_ref, out_ref):
    owned = coef_ref.shape[0]
    scale = -coef_ref[...]
    total = t_ref[0].astype(F32)
    for s in range(1, t_ref.shape[0]):
        total = total + t_ref[s].astype(F32)
    row = lax.broadcasted_iota(jnp.int32, (8, LANES), 0)
    atom_id = lax.broadcasted_iota(jnp.int32, (LANES, LANES), 0)
    terms = [total[:, x * LANES : (x + 1) * LANES] * scale for x in range(3)]
    values, hits = [], []
    for b in range(owned):
        value = jnp.zeros((8, LANES), F32)
        for x in range(3):
            value = jnp.where(row == x, terms[x][b : b + 1], value)
        values.append(value)
        hits.append(jnp.where(atom_ref[b : b + 1, :] == atom_id, 1.0, 0.0).astype(BF))
    value = jnp.concatenate(values, axis=1)
    high = value.astype(BF)
    low = (value - high.astype(F32)).astype(BF)
    sums = contract(jnp.concatenate([high, low], axis=0), jnp.concatenate(hits, axis=1))
    out = sums[:8] + sums[8:]
    for d in range(out_ref.shape[0]):
        out_ref[d] = out


def forces(solution, proj_vals, slot_offset, slot_block, proj_coef, pole_weight, proj_atom):
    _, cols, planes, ny, nz = solution.shape
    slots, proj, win = proj_vals.shape
    bricks = lax.axis_size("grid")
    owned = proj_coef.shape[0]
    rows = planes * ny * nz // LANES
    per_plane = rows // planes
    per = cols // bricks
    brick = lax.axis_index("grid").astype(jnp.int32)
    x = pltpu.with_memory_space_constraint(solution.reshape(cols, planes, ny, nz), pltpu.HBM)
    proj_vals = pltpu.with_memory_space_constraint(proj_vals, pltpu.HBM)
    slot_offset = pltpu.with_memory_space_constraint(slot_offset, pltpu.HBM)

    def params(mib):
        return pltpu.CompilerParams(vmem_limit_bytes=mib << 20)

    smem = pl.BlockSpec(memory_space=pltpu.SMEM)
    vmem = pl.BlockSpec(memory_space=pltpu.VMEM)
    hbm = pl.BlockSpec(memory_space=pltpu.HBM)

    dma = pltpu.SemaphoreType.DMA
    xr, lo, hi, c_part = pl.pallas_call(
        value_kernel,
        out_shape=(
            jax.ShapeDtypeStruct((rows, cols, LANES), BF),
            jax.ShapeDtypeStruct((per_plane, cols, LANES), BF),
            jax.ShapeDtypeStruct((per_plane, cols, LANES), BF),
            jax.ShapeDtypeStruct((bricks, slots, per * LANES), BF),
        ),
        in_specs=[hbm, hbm, hbm],
        out_specs=[hbm, hbm, hbm, vmem],
        scratch_shapes=[
            pltpu.SMEM((slots,), jnp.int32),
            pltpu.VMEM((cols, planes, ny, nz), BF),
            pltpu.VMEM((slots, proj, win), BF),
            pltpu.VMEM((rows, cols, LANES), BF),
            pltpu.VMEM((planes, nz // LANES, GROUP_COLS * ny, LANES), F32),
            pltpu.VMEM((slots * cols, LANES), F32),
            dma,
            dma((cols // GROUP_COLS,)),
            dma((slots,)),
            dma((3,)),
        ],
        compiler_params=params(LIMIT),
        name="values",
    )(slot_offset, x, proj_vals)

    arrived = lax.all_to_all(c_part, "grid", 0, 0, tiled=True)

    up = [(i, (i + 1) % bricks) for i in range(bricks)]
    down = [(j, i) for i, j in up]
    before = lax.ppermute(hi, "grid", up)
    after = lax.ppermute(lo, "grid", down)

    def scratch(fields):
        return [
            pltpu.SMEM((slots,), jnp.int32),
            pltpu.VMEM((rows, cols, LANES), BF),
            pltpu.VMEM((rows, fields * cols, LANES), BF),
            pltpu.VMEM((slots, proj, win), BF),
            dma,
            dma,
            dma((slots,)),
        ]

    e_yz = pl.pallas_call(
        inside_kernel,
        out_shape=jax.ShapeDtypeStruct((slots, 2 * cols, LANES), BF),
        in_specs=[hbm] * 3,
        out_specs=vmem,
        scratch_shapes=scratch(2),
        compiler_params=params(LIMIT),
        name="inside",
    )(slot_offset, xr, proj_vals)

    arrived, e_yz = lax.optimization_barrier((arrived, e_yz))
    ids = slot_block.reshape(-1)
    same = (ids[:, None] == ids[None, :]).astype(BF)
    summed = jnp.dot(
        same, arrived.reshape(bricks * slots, per * LANES), preferred_element_type=F32
    ).astype(BF)
    coefs = lax.all_to_all(
        summed.reshape(bricks, slots, per * LANES), "grid", 0, 0, tiled=True
    )

    e_x = pl.pallas_call(
        across_kernel,
        out_shape=jax.ShapeDtypeStruct((slots, cols, LANES), BF),
        in_specs=[hbm, hbm, vmem, vmem, hbm],
        out_specs=vmem,
        scratch_shapes=scratch(1),
        compiler_params=params(LIMIT),
        name="across",
    )(slot_offset, xr, before, after, proj_vals)

    terms = pl.pallas_call(
        term_kernel,
        out_shape=jax.ShapeDtypeStruct((bricks, owned, 3 * LANES), BF),
        in_specs=[smem, smem, smem, vmem, vmem, vmem],
        out_specs=vmem,
        scratch_shapes=[
            pltpu.VMEM((slots * cols, LANES), F32),
            pltpu.VMEM((bricks, owned, 3 * LANES), F32),
        ],
        compiler_params=params(8),
        name="terms",
    )(slot_block, brick[None], pole_weight, coefs, e_x, e_yz)

    at_owner = lax.all_to_all(terms, "grid", 0, 0, tiled=True)
    copies = lax.axis_size("band") * lax.axis_size("pole")
    shares = pl.pallas_call(
        owner_kernel,
        out_shape=jax.ShapeDtypeStruct((copies, 8, LANES), F32),
        compiler_params=params(4),
        name="owner",
    )(at_owner, proj_coef, proj_atom)
    gathered = lax.all_to_all(shares, ("band", "pole"), 0, 0, tiled=True)
    return jnp.sum(gathered[:, :3, :ATOM_OWN], axis=0)


def solution(mesh):
    placed = (
        P("pole", "band", "grid", None, None),
        P("grid", None, None),
        P("grid"),
        P(),
        P("grid", None),
        P("pole"),
        P("grid", None),
    )
    return jax.shard_map(
        forces, mesh=mesh, in_specs=placed, out_specs=P(None, "grid"), check_vma=False
    )
```

```python
import jax
import jax.numpy as jnp
from jax import lax
from jax.experimental import pallas as pl
from jax.experimental.pallas import tpu as pltpu
from jax.sharding import PartitionSpec as P

ATOM_OWN = 56
LANES = 128
BF = jnp.bfloat16
LIMIT = 24
NY = 16
GROUP = 4
VALUE_GROUP = 4
AHEAD = 12
GROUP_COLS = 16
F32 = jnp.float32


def shifted(block, shift, chunks):
    lane = lax.broadcasted_iota(jnp.int32, (block.shape[0], LANES), 1)
    low = lane < shift
    rolled = [
        pltpu.roll(block[:, j * LANES : (j + 1) * LANES], shift, 1) for j in range(chunks)
    ]
    zero = jnp.zeros_like(rolled[0])
    pieces = [jnp.where(low, zero, rolled[0])]
    for j in range(1, chunks):
        pieces.append(jnp.where(low, rolled[j - 1], rolled[j]))
    pieces.append(jnp.where(low, rolled[-1], zero))
    return jnp.concatenate(pieces, axis=1)


def window_of(field_ref, first, chunks):
    last = field_ref.shape[0] - 1
    parts = [field_ref[first + j] for j in range(chunks - 1)]
    parts.append(field_ref[jnp.minimum(first + chunks - 1, last)])
    return jnp.concatenate(parts, axis=1)


def contract(a, b):
    return lax.dot_general(a, b, (((1,), (1,)), ((), ())), preferred_element_type=F32)


def value_kernel(
    off_hbm, x_hbm, p_hbm, xr_hbm, lo_hbm, hi_hbm, c_ref, off, xbuf, pbuf, xr, stage, c32, osem, xsem, psem, rsem
):
    cols, planes, ny, nz = xbuf.shape
    slots = pbuf.shape[0]
    halves = nz // LANES
    chunks = pbuf.shape[2] // LANES
    per_plane = ny * halves

    def x_copy(g):
        part = pl.ds(g * GROUP_COLS, GROUP_COLS)
        return pltpu.make_async_copy(x_hbm.at[part], xbuf.at[part], xsem.at[g])

    def p_copy(k):
        return pltpu.make_async_copy(p_hbm.at[k], pbuf.at[k], psem.at[k])

    def plane(x):
        return pl.ds(x * per_plane, per_plane)

    for g in range(cols // GROUP_COLS):
        x_copy(g).start()
    off_copy = pltpu.make_async_copy(off_hbm, off, osem)
    off_copy.start()
    outgoing = [
        pltpu.make_async_copy(xr, xr_hbm, rsem.at[0]),
        pltpu.make_async_copy(xr.at[plane(0)], lo_hbm, rsem.at[1]),
        pltpu.make_async_copy(xr.at[plane(planes - 1)], hi_hbm, rsem.at[2]),
    ]
    for g in range(cols // GROUP_COLS):
        x_copy(g).wait()
        for k in range(g * slots * GROUP_COLS // cols, (g + 1) * slots * GROUP_COLS // cols):
            p_copy(k).start()
        part = slice(g * GROUP_COLS, (g + 1) * GROUP_COLS)
        for x in range(planes):
            for half in range(halves):
                piece = xbuf[part, x, :, half * LANES : (half + 1) * LANES].astype(F32)
                stage[x, half] = piece.reshape(GROUP_COLS * ny, LANES)
                for y in range(ny):
                    row = stage[x, half, pl.ds(y, GROUP_COLS, stride=ny), :].astype(BF)
                    xr[(x * ny + y) * halves + half, part] = row
    for copy in outgoing:
        copy.start()
    off_copy.wait()

    def group(i, carry):
        for u in range(VALUE_GROUP):
            p_copy(i * VALUE_GROUP + u).wait()

        for u in range(VALUE_GROUP):
            k = i * VALUE_GROUP + u
            proj = shifted(pbuf[k], off[k] & (LANES - 1), chunks)
            field = window_of(xr, off[k] >> 7, chunks + 1)
            c32[pl.ds(pl.multiple_of(k * cols, cols), cols), :] = contract(field, proj)
        return carry

    lax.fori_loop(0, slots // VALUE_GROUP, group, 0)

    dests = c_ref.shape[0]
    per = cols // dests
    for j in range(cols):
        row = c32[pl.ds(j, dests, stride=cols), :]
        c_ref[j // per, :, (j % per) * LANES : (j % per + 1) * LANES] = row.astype(BF)
    for copy in outgoing:
        copy.wait()


def fetch_blocks(off_hbm, off, p_hbm, pbuf, osem, psem):
    copies = [
        pltpu.make_async_copy(p_hbm.at[k], pbuf.at[k], psem.at[k]) for k in range(AHEAD)
    ]
    offsets = pltpu.make_async_copy(off_hbm, off, osem)
    offsets.start()
    for copy in copies:
        copy.start()
    return offsets


def partials(off, p_hbm, pbuf, psem, fields, e_ref):
    slots, _, win = pbuf.shape
    chunks = win // LANES

    def p_copy(k):
        return pltpu.make_async_copy(p_hbm.at[k], pbuf.at[k], psem.at[k])

    def group(i, carry):
        for u in range(GROUP):
            p_copy(i * GROUP + u).wait()

        @pl.when(i * GROUP + AHEAD < slots)
        def _():
            for u in range(GROUP):
                p_copy(i * GROUP + u + AHEAD).start()

        for u in range(GROUP):
            k = i * GROUP + u
            proj = shifted(pbuf[k], off[k] & (LANES - 1), chunks)
            field = window_of(fields, off[k] >> 7, chunks + 1)
            e_ref[k] = contract(field, proj).astype(BF)
        return carry

    lax.fori_loop(0, slots // GROUP, group, 0)


def inside_kernel(off_hbm, xr_hbm, p_hbm, e_ref, off, xr, fields, pbuf, osem, xsem, psem):
    rows, cols, _ = xr.shape
    xr_copy = pltpu.make_async_copy(xr_hbm, xr, xsem)
    xr_copy.start()
    offsets = fetch_blocks(off_hbm, off, p_hbm, pbuf, osem, psem)
    lane = lax.broadcasted_iota(jnp.int32, (cols, LANES), 1)
    last = lane == LANES - 1
    first = lane == 0

    def pair(r, carry):
        y = r % NY
        up = 2 * (r - y + (y + 1) % NY)
        down = 2 * (r - y + (y + NY - 1) % NY)
        h = 2 * r
        for half in range(2):
            fields[h + half, :cols] = xr[up + half] - xr[down + half]
        a = xr[h]
        b = xr[h + 1]
        a_up = pltpu.roll(a, LANES - 1, 1)
        b_up = pltpu.roll(b, LANES - 1, 1)
        a_down = pltpu.roll(a, 1, 1)
        b_down = pltpu.roll(b, 1, 1)
        fields[h, cols:] = jnp.where(last, b_up, a_up) - jnp.where(first, b_down, a_down)
        fields[h + 1, cols:] = jnp.where(last, a_up, b_up) - jnp.where(first, a_down, b_down)
        return carry

    xr_copy.wait()
    lax.fori_loop(0, rows // 2, pair, 0, unroll=4)
    offsets.wait()
    partials(off, p_hbm, pbuf, psem, fields, e_ref)


def across_kernel(
    off_hbm, xr_hbm, before_ref, after_ref, p_hbm, e_ref, off, xr, fields, pbuf, osem, xsem, psem
):
    rows = xr.shape[0]
    per_plane = before_ref.shape[0]
    xr_copy = pltpu.make_async_copy(xr_hbm, xr, xsem)
    xr_copy.start()
    offsets = fetch_blocks(off_hbm, off, p_hbm, pbuf, osem, psem)

    def inner(h, carry):
        fields[h] = xr[h + per_plane] - xr[h - per_plane]
        return carry

    def edge(h, carry):
        fields[h] = xr[h + per_plane] - before_ref[h]
        t = rows - per_plane + h
        fields[t] = after_ref[h] - xr[t - per_plane]
        return carry

    xr_copy.wait()
    lax.fori_loop(per_plane, rows - per_plane, inner, 0, unroll=8)
    lax.fori_loop(0, per_plane, edge, 0, unroll=8)
    offsets.wait()
    partials(off, p_hbm, pbuf, psem, fields, e_ref)


def term_kernel(blk_ref, brick_ref, w_ref, c_ref, ex_ref, eyz_ref, out_ref, c32, t_ref):
    dests, slots, _ = c_ref.shape
    cols = ex_ref.shape[1]
    per = cols // dests
    for j in range(cols):
        c = c_ref[j // per, :, (j % per) * LANES : (j % per + 1) * LANES].astype(F32)
        c32[pl.ds(j, slots, stride=cols), :] = c
    t_ref[...] = jnp.zeros(t_ref.shape, F32)
    owned = t_ref.shape[1]
    brick = brick_ref[0]
    w = w_ref[0]
    place = lax.broadcasted_iota(jnp.int32, (owned, LANES), 0)
    for k in range(slots):
        c = c32[k * cols : (k + 1) * cols] * w
        g = blk_ref[brick, k]
        o = g // owned
        here = place == g % owned
        parts = (ex_ref[k], eyz_ref[k, :cols], eyz_ref[k, cols:])
        for x in range(3):
            term = jnp.sum(c * parts[x].astype(F32), axis=0, keepdims=True)
            at = slice(x * LANES, (x + 1) * LANES)
            t_ref[o, :, at] = t_ref[o, :, at] + jnp.where(here, term, 0.0)
    out_ref[...] = t_ref[...].astype(BF)


def owner_kernel(t_ref, coef_ref, atom_ref, out_ref):
    owned = coef_ref.shape[0]
    scale = -coef_ref[...]
    total = t_ref[0].astype(F32)
    for s in range(1, t_ref.shape[0]):
        total = total + t_ref[s].astype(F32)
    row = lax.broadcasted_iota(jnp.int32, (8, LANES), 0)
    atom_id = lax.broadcasted_iota(jnp.int32, (LANES, LANES), 0)
    terms = [total[:, x * LANES : (x + 1) * LANES] * scale for x in range(3)]
    values, hits = [], []
    for b in range(owned):
        value = jnp.zeros((8, LANES), F32)
        for x in range(3):
            value = jnp.where(row == x, terms[x][b : b + 1], value)
        values.append(value)
        hits.append(jnp.where(atom_ref[b : b + 1, :] == atom_id, 1.0, 0.0).astype(BF))
    value = jnp.concatenate(values, axis=1)
    high = value.astype(BF)
    low = (value - high.astype(F32)).astype(BF)
    sums = contract(jnp.concatenate([high, low], axis=0), jnp.concatenate(hits, axis=1))
    out = sums[:8] + sums[8:]
    for d in range(out_ref.shape[0]):
        out_ref[d] = out


def forces(solution, proj_vals, slot_offset, slot_block, proj_coef, pole_weight, proj_atom):
    _, cols, planes, ny, nz = solution.shape
    slots, proj, win = proj_vals.shape
    bricks = lax.axis_size("grid")
    owned = proj_coef.shape[0]
    rows = planes * ny * nz // LANES
    per_plane = rows // planes
    per = cols // bricks
    brick = lax.axis_index("grid").astype(jnp.int32)
    x = pltpu.with_memory_space_constraint(solution.reshape(cols, planes, ny, nz), pltpu.HBM)
    proj_vals = pltpu.with_memory_space_constraint(proj_vals, pltpu.HBM)
    slot_offset = pltpu.with_memory_space_constraint(slot_offset, pltpu.HBM)

    def params(mib):
        return pltpu.CompilerParams(vmem_limit_bytes=mib << 20)

    smem = pl.BlockSpec(memory_space=pltpu.SMEM)
    vmem = pl.BlockSpec(memory_space=pltpu.VMEM)
    hbm = pl.BlockSpec(memory_space=pltpu.HBM)

    dma = pltpu.SemaphoreType.DMA
    xr, lo, hi, c_part = pl.pallas_call(
        value_kernel,
        out_shape=(
            jax.ShapeDtypeStruct((rows, cols, LANES), BF),
            jax.ShapeDtypeStruct((per_plane, cols, LANES), BF),
            jax.ShapeDtypeStruct((per_plane, cols, LANES), BF),
            jax.ShapeDtypeStruct((bricks, slots, per * LANES), BF),
        ),
        in_specs=[hbm, hbm, hbm],
        out_specs=[hbm, hbm, hbm, vmem],
        scratch_shapes=[
            pltpu.SMEM((slots,), jnp.int32),
            pltpu.VMEM((cols, planes, ny, nz), BF),
            pltpu.VMEM((slots, proj, win), BF),
            pltpu.VMEM((rows, cols, LANES), BF),
            pltpu.VMEM((planes, nz // LANES, GROUP_COLS * ny, LANES), F32),
            pltpu.VMEM((slots * cols, LANES), F32),
            dma,
            dma((cols // GROUP_COLS,)),
            dma((slots,)),
            dma((3,)),
        ],
        compiler_params=params(LIMIT),
        name="values",
    )(slot_offset, x, proj_vals)

    arrived = lax.all_to_all(c_part, "grid", 0, 0, tiled=True)

    up = [(i, (i + 1) % bricks) for i in range(bricks)]
    down = [(j, i) for i, j in up]
    before = lax.ppermute(hi, "grid", up)
    after = lax.ppermute(lo, "grid", down)

    def scratch(fields):
        return [
            pltpu.SMEM((slots,), jnp.int32),
            pltpu.VMEM((rows, cols, LANES), BF),
            pltpu.VMEM((rows, fields * cols, LANES), BF),
            pltpu.VMEM((slots, proj, win), BF),
            dma,
            dma,
            dma((slots,)),
        ]

    e_yz = pl.pallas_call(
        inside_kernel,
        out_shape=jax.ShapeDtypeStruct((slots, 2 * cols, LANES), BF),
        in_specs=[hbm] * 3,
        out_specs=vmem,
        scratch_shapes=scratch(2),
        compiler_params=params(LIMIT),
        name="inside",
    )(slot_offset, xr, proj_vals)

    arrived, e_yz = lax.optimization_barrier((arrived, e_yz))
    ids = slot_block.reshape(-1)
    same = (ids[:, None] == ids[None, :]).astype(BF)
    summed = jnp.dot(
        same, arrived.reshape(bricks * slots, per * LANES), preferred_element_type=F32
    ).astype(BF)
    coefs = lax.all_to_all(
        summed.reshape(bricks, slots, per * LANES), "grid", 0, 0, tiled=True
    )

    e_x = pl.pallas_call(
        across_kernel,
        out_shape=jax.ShapeDtypeStruct((slots, cols, LANES), BF),
        in_specs=[hbm, hbm, vmem, vmem, hbm],
        out_specs=vmem,
        scratch_shapes=scratch(1),
        compiler_params=params(LIMIT),
        name="across",
    )(slot_offset, xr, before, after, proj_vals)

    terms = pl.pallas_call(
        term_kernel,
        out_shape=jax.ShapeDtypeStruct((bricks, owned, 3 * LANES), BF),
        in_specs=[smem, smem, smem, vmem, vmem, vmem],
        out_specs=vmem,
        scratch_shapes=[
            pltpu.VMEM((slots * cols, LANES), F32),
            pltpu.VMEM((bricks, owned, 3 * LANES), F32),
        ],
        compiler_params=params(8),
        name="terms",
    )(slot_block, brick[None], pole_weight, coefs, e_x, e_yz)

    at_owner = lax.all_to_all(terms, "grid", 0, 0, tiled=True)
    copies = lax.axis_size("band") * lax.axis_size("pole")
    shares = pl.pallas_call(
        owner_kernel,
        out_shape=jax.ShapeDtypeStruct((copies, 8, LANES), F32),
        compiler_params=params(4),
        name="owner",
    )(at_owner, proj_coef, proj_atom)
    gathered = lax.all_to_all(shares, ("band", "pole"), 0, 0, tiled=True)
    return jnp.sum(gathered[:, :3, :ATOM_OWN], axis=0)


def solution(mesh):
    placed = (
        P("pole", "band", "grid", None, None),
        P("grid", None, None),
        P("grid"),
        P(),
        P("grid", None),
        P("pole"),
        P("grid", None),
    )
    return jax.shard_map(
        forces, mesh=mesh, in_specs=placed, out_specs=P(None, "grid"), check_vma=False
    )
```

```python
import jax
import jax.numpy as jnp
from jax import lax
from jax.experimental import pallas as pl
from jax.experimental.pallas import tpu as pltpu
from jax.sharding import PartitionSpec as P

ATOM_OWN = 56
LANES = 128
BF = jnp.bfloat16
LIMIT = 24
NY = 16
GROUP = 4
VALUE_GROUP = 4
AHEAD = 12
GROUP_COLS = 16
F32 = jnp.float32


def shifted(block, shift, chunks):
    lane = lax.broadcasted_iota(jnp.int32, (block.shape[0], LANES), 1)
    low = lane < shift
    rolled = [
        pltpu.roll(block[:, j * LANES : (j + 1) * LANES], shift, 1) for j in range(chunks)
    ]
    zero = jnp.zeros_like(rolled[0])
    pieces = [jnp.where(low, zero, rolled[0])]
    for j in range(1, chunks):
        pieces.append(jnp.where(low, rolled[j - 1], rolled[j]))
    pieces.append(jnp.where(low, rolled[-1], zero))
    return jnp.concatenate(pieces, axis=1)


def window_of(field_ref, first, chunks):
    last = field_ref.shape[0] - 1
    parts = [field_ref[first + j] for j in range(chunks - 1)]
    parts.append(field_ref[jnp.minimum(first + chunks - 1, last)])
    return jnp.concatenate(parts, axis=1)


def contract(a, b):
    return lax.dot_general(a, b, (((1,), (1,)), ((), ())), preferred_element_type=F32)


def value_kernel(
    off_hbm, x_hbm, p_hbm, xr_hbm, lo_hbm, hi_hbm, c_ref, off, xbuf, pbuf, xr, stage, c32, osem, xsem, psem, rsem
):
    cols, planes, ny, nz = xbuf.shape
    slots = pbuf.shape[0]
    halves = nz // LANES
    chunks = pbuf.shape[2] // LANES
    per_plane = ny * halves

    def x_copy(g):
        part = pl.ds(g * GROUP_COLS, GROUP_COLS)
        return pltpu.make_async_copy(x_hbm.at[part], xbuf.at[part], xsem.at[g])

    def p_copy(k):
        return pltpu.make_async_copy(p_hbm.at[k], pbuf.at[k], psem.at[k])

    def plane(x):
        return pl.ds(x * per_plane, per_plane)

    for g in range(cols // GROUP_COLS):
        x_copy(g).start()
    off_copy = pltpu.make_async_copy(off_hbm, off, osem)
    off_copy.start()
    outgoing = [
        pltpu.make_async_copy(xr, xr_hbm, rsem.at[0]),
        pltpu.make_async_copy(xr.at[plane(0)], lo_hbm, rsem.at[1]),
        pltpu.make_async_copy(xr.at[plane(planes - 1)], hi_hbm, rsem.at[2]),
    ]
    for g in range(cols // GROUP_COLS):
        x_copy(g).wait()
        for k in range(g * slots * GROUP_COLS // cols, (g + 1) * slots * GROUP_COLS // cols):
            p_copy(k).start()
        part = slice(g * GROUP_COLS, (g + 1) * GROUP_COLS)
        for x in range(planes):
            for half in range(halves):
                piece = xbuf[part, x, :, half * LANES : (half + 1) * LANES].astype(F32)
                stage[x, half] = piece.reshape(GROUP_COLS * ny, LANES)
                for y in range(ny):
                    row = stage[x, half, pl.ds(y, GROUP_COLS, stride=ny), :].astype(BF)
                    xr[(x * ny + y) * halves + half, part] = row
    for copy in outgoing:
        copy.start()
    off_copy.wait()

    def group(i, carry):
        for u in range(VALUE_GROUP):
            p_copy(i * VALUE_GROUP + u).wait()

        for u in range(VALUE_GROUP):
            k = i * VALUE_GROUP + u
            proj = shifted(pbuf[k], off[k] & (LANES - 1), chunks)
            field = window_of(xr, off[k] >> 7, chunks + 1)
            c32[pl.ds(pl.multiple_of(k * cols, cols), cols), :] = contract(field, proj)
        return carry

    lax.fori_loop(0, slots // VALUE_GROUP, group, 0)

    dests = c_ref.shape[0]
    per = cols // dests
    for j in range(cols):
        row = c32[pl.ds(j, dests, stride=cols), :]
        c_ref[j // per, :, (j % per) * LANES : (j % per + 1) * LANES] = row.astype(BF)
    for copy in outgoing:
        copy.wait()


def fetch_blocks(off_hbm, off, p_hbm, pbuf, osem, psem):
    copies = [
        pltpu.make_async_copy(p_hbm.at[k], pbuf.at[k], psem.at[k]) for k in range(AHEAD)
    ]
    offsets = pltpu.make_async_copy(off_hbm, off, osem)
    offsets.start()
    for copy in copies:
        copy.start()
    return offsets


def partials(off, p_hbm, pbuf, psem, fields, e_ref):
    slots, _, win = pbuf.shape
    chunks = win // LANES

    def p_copy(k):
        return pltpu.make_async_copy(p_hbm.at[k], pbuf.at[k], psem.at[k])

    def group(i, carry):
        for u in range(GROUP):
            p_copy(i * GROUP + u).wait()

        @pl.when(i * GROUP + AHEAD < slots)
        def _():
            for u in range(GROUP):
                p_copy(i * GROUP + u + AHEAD).start()

        for u in range(GROUP):
            k = i * GROUP + u
            proj = shifted(pbuf[k], off[k] & (LANES - 1), chunks)
            field = window_of(fields, off[k] >> 7, chunks + 1)
            e_ref[k] = contract(field, proj).astype(BF)
        return carry

    lax.fori_loop(0, slots // GROUP, group, 0)


def inside_kernel(off_hbm, xr, p_hbm, e_ref, off, fields, pbuf, osem, psem):
    rows, cols, _ = xr.shape
    offsets = fetch_blocks(off_hbm, off, p_hbm, pbuf, osem, psem)
    lane = lax.broadcasted_iota(jnp.int32, (cols, LANES), 1)
    last = lane == LANES - 1
    first = lane == 0

    def pair(r, carry):
        y = r % NY
        up = 2 * (r - y + (y + 1) % NY)
        down = 2 * (r - y + (y + NY - 1) % NY)
        h = 2 * r
        for half in range(2):
            fields[h + half, :cols] = xr[up + half] - xr[down + half]
        a = xr[h]
        b = xr[h + 1]
        a_up = pltpu.roll(a, LANES - 1, 1)
        b_up = pltpu.roll(b, LANES - 1, 1)
        a_down = pltpu.roll(a, 1, 1)
        b_down = pltpu.roll(b, 1, 1)
        fields[h, cols:] = jnp.where(last, b_up, a_up) - jnp.where(first, b_down, a_down)
        fields[h + 1, cols:] = jnp.where(last, a_up, b_up) - jnp.where(first, a_down, b_down)
        return carry

    lax.fori_loop(0, rows // 2, pair, 0, unroll=4)
    offsets.wait()
    partials(off, p_hbm, pbuf, psem, fields, e_ref)


def across_kernel(
    off_hbm, xr, before_ref, after_ref, p_hbm, e_ref, off, fields, pbuf, osem, psem
):
    rows = xr.shape[0]
    per_plane = before_ref.shape[0]
    offsets = fetch_blocks(off_hbm, off, p_hbm, pbuf, osem, psem)

    def inner(h, carry):
        fields[h] = xr[h + per_plane] - xr[h - per_plane]
        return carry

    def edge(h, carry):
        fields[h] = xr[h + per_plane] - before_ref[h]
        t = rows - per_plane + h
        fields[t] = after_ref[h] - xr[t - per_plane]
        return carry

    lax.fori_loop(per_plane, rows - per_plane, inner, 0, unroll=8)
    lax.fori_loop(0, per_plane, edge, 0, unroll=8)
    offsets.wait()
    partials(off, p_hbm, pbuf, psem, fields, e_ref)


def term_kernel(blk_ref, brick_ref, w_ref, c_ref, ex_ref, eyz_ref, out_ref, c32, t_ref):
    dests, slots, _ = c_ref.shape
    cols = ex_ref.shape[1]
    per = cols // dests
    for j in range(cols):
        c = c_ref[j // per, :, (j % per) * LANES : (j % per + 1) * LANES].astype(F32)
        c32[pl.ds(j, slots, stride=cols), :] = c
    t_ref[...] = jnp.zeros(t_ref.shape, F32)
    owned = t_ref.shape[1]
    brick = brick_ref[0]
    w = w_ref[0]
    place = lax.broadcasted_iota(jnp.int32, (owned, LANES), 0)
    for k in range(slots):
        c = c32[k * cols : (k + 1) * cols] * w
        g = blk_ref[brick, k]
        o = g // owned
        here = place == g % owned
        parts = (ex_ref[k], eyz_ref[k, :cols], eyz_ref[k, cols:])
        for x in range(3):
            term = jnp.sum(c * parts[x].astype(F32), axis=0, keepdims=True)
            at = slice(x * LANES, (x + 1) * LANES)
            t_ref[o, :, at] = t_ref[o, :, at] + jnp.where(here, term, 0.0)
    out_ref[...] = t_ref[...].astype(BF)


def owner_kernel(t_ref, coef_ref, atom_ref, out_ref):
    owned = coef_ref.shape[0]
    scale = -coef_ref[...]
    total = t_ref[0].astype(F32)
    for s in range(1, t_ref.shape[0]):
        total = total + t_ref[s].astype(F32)
    row = lax.broadcasted_iota(jnp.int32, (8, LANES), 0)
    atom_id = lax.broadcasted_iota(jnp.int32, (LANES, LANES), 0)
    terms = [total[:, x * LANES : (x + 1) * LANES] * scale for x in range(3)]
    values, hits = [], []
    for b in range(owned):
        value = jnp.zeros((8, LANES), F32)
        for x in range(3):
            value = jnp.where(row == x, terms[x][b : b + 1], value)
        values.append(value)
        hits.append(jnp.where(atom_ref[b : b + 1, :] == atom_id, 1.0, 0.0).astype(BF))
    value = jnp.concatenate(values, axis=1)
    high = value.astype(BF)
    low = (value - high.astype(F32)).astype(BF)
    sums = contract(jnp.concatenate([high, low], axis=0), jnp.concatenate(hits, axis=1))
    out = sums[:8] + sums[8:]
    for d in range(out_ref.shape[0]):
        out_ref[d] = out


def forces(solution, proj_vals, slot_offset, slot_block, proj_coef, pole_weight, proj_atom):
    _, cols, planes, ny, nz = solution.shape
    slots, proj, win = proj_vals.shape
    bricks = lax.axis_size("grid")
    owned = proj_coef.shape[0]
    rows = planes * ny * nz // LANES
    per_plane = rows // planes
    per = cols // bricks
    brick = lax.axis_index("grid").astype(jnp.int32)
    x = pltpu.with_memory_space_constraint(solution.reshape(cols, planes, ny, nz), pltpu.HBM)
    proj_vals = pltpu.with_memory_space_constraint(proj_vals, pltpu.HBM)
    slot_offset = pltpu.with_memory_space_constraint(slot_offset, pltpu.HBM)

    def params(mib):
        return pltpu.CompilerParams(vmem_limit_bytes=mib << 20)

    smem = pl.BlockSpec(memory_space=pltpu.SMEM)
    vmem = pl.BlockSpec(memory_space=pltpu.VMEM)
    hbm = pl.BlockSpec(memory_space=pltpu.HBM)

    dma = pltpu.SemaphoreType.DMA
    xr, lo, hi, c_part = pl.pallas_call(
        value_kernel,
        out_shape=(
            jax.ShapeDtypeStruct((rows, cols, LANES), BF),
            jax.ShapeDtypeStruct((per_plane, cols, LANES), BF),
            jax.ShapeDtypeStruct((per_plane, cols, LANES), BF),
            jax.ShapeDtypeStruct((bricks, slots, per * LANES), BF),
        ),
        in_specs=[hbm, hbm, hbm],
        out_specs=[hbm, hbm, hbm, vmem],
        scratch_shapes=[
            pltpu.SMEM((slots,), jnp.int32),
            pltpu.VMEM((cols, planes, ny, nz), BF),
            pltpu.VMEM((slots, proj, win), BF),
            pltpu.VMEM((rows, cols, LANES), BF),
            pltpu.VMEM((planes, nz // LANES, GROUP_COLS * ny, LANES), F32),
            pltpu.VMEM((slots * cols, LANES), F32),
            dma,
            dma((cols // GROUP_COLS,)),
            dma((slots,)),
            dma((3,)),
        ],
        compiler_params=params(LIMIT),
        name="values",
    )(slot_offset, x, proj_vals)

    arrived = lax.all_to_all(c_part, "grid", 0, 0, tiled=True)

    up = [(i, (i + 1) % bricks) for i in range(bricks)]
    down = [(j, i) for i, j in up]
    before = lax.ppermute(hi, "grid", up)
    after = lax.ppermute(lo, "grid", down)

    def scratch(fields):
        return [
            pltpu.SMEM((slots,), jnp.int32),
            pltpu.VMEM((rows, fields * cols, LANES), BF),
            pltpu.VMEM((slots, proj, win), BF),
            dma,
            dma((slots,)),
        ]

    e_yz = pl.pallas_call(
        inside_kernel,
        out_shape=jax.ShapeDtypeStruct((slots, 2 * cols, LANES), BF),
        in_specs=[hbm, vmem, hbm],
        out_specs=vmem,
        scratch_shapes=scratch(2),
        compiler_params=params(LIMIT),
        name="inside",
    )(slot_offset, xr, proj_vals)

    arrived, e_yz = lax.optimization_barrier((arrived, e_yz))
    ids = slot_block.reshape(-1)
    same = (ids[:, None] == ids[None, :]).astype(BF)
    summed = jnp.dot(
        same, arrived.reshape(bricks * slots, per * LANES), preferred_element_type=F32
    ).astype(BF)
    coefs = lax.all_to_all(
        summed.reshape(bricks, slots, per * LANES), "grid", 0, 0, tiled=True
    )

    e_x = pl.pallas_call(
        across_kernel,
        out_shape=jax.ShapeDtypeStruct((slots, cols, LANES), BF),
        in_specs=[hbm, vmem, vmem, vmem, hbm],
        out_specs=vmem,
        scratch_shapes=scratch(1),
        compiler_params=params(LIMIT),
        name="across",
    )(slot_offset, xr, before, after, proj_vals)

    terms = pl.pallas_call(
        term_kernel,
        out_shape=jax.ShapeDtypeStruct((bricks, owned, 3 * LANES), BF),
        in_specs=[smem, smem, smem, vmem, vmem, vmem],
        out_specs=vmem,
        scratch_shapes=[
            pltpu.VMEM((slots * cols, LANES), F32),
            pltpu.VMEM((bricks, owned, 3 * LANES), F32),
        ],
        compiler_params=params(8),
        name="terms",
    )(slot_block, brick[None], pole_weight, coefs, e_x, e_yz)

    at_owner = lax.all_to_all(terms, "grid", 0, 0, tiled=True)
    copies = lax.axis_size("band") * lax.axis_size("pole")
    shares = pl.pallas_call(
        owner_kernel,
        out_shape=jax.ShapeDtypeStruct((copies, 8, LANES), F32),
        compiler_params=params(4),
        name="owner",
    )(at_owner, proj_coef, proj_atom)
    gathered = lax.all_to_all(shares, ("band", "pole"), 0, 0, tiled=True)
    return jnp.sum(gathered[:, :3, :ATOM_OWN], axis=0)


def solution(mesh):
    placed = (
        P("pole", "band", "grid", None, None),
        P("grid", None, None),
        P("grid"),
        P(),
        P("grid", None),
        P("pole"),
        P("grid", None),
    )
    return jax.shard_map(
        forces, mesh=mesh, in_specs=placed, out_specs=P(None, "grid"), check_vma=False
    )
```
